32 devices in a mesh: groups: 2 (over y), chan: 4 (over z), tm: 2 (over core), dp: 2 (over x).
Axes of the slice: x: 2, y: 2, z: 4, core: 2. Of those that a mesh axis runs over, the one named last changes fastest.
Arguments:
- features: bfloat16 [384, 4, 8, 256], P('chan', ('groups', 'dp'), 'tm'), parts along dimension 1, may hold values from -6 to 6
- kernel: bfloat16 [384, 27, 384], P('chan'), may hold values from -0.078125 to 0.078125
- cotangent: bfloat16 [384, 4, 8, 256], P('chan', ('groups', 'dp'), 'tm'), parts along dimension 1, may hold values from -6 to 6
Outputs:
- conv_out: bfloat16 [384, 4, 8, 256], P('chan', ('groups', 'dp'), 'tm'), parts along dimension 1
- feature_grad: bfloat16 [384, 4, 8, 256], P('chan', ('groups', 'dp'), 'tm'), parts along dimension 1
- kernel_grad: float32 [768, 27, 384], P(('groups', 'chan')), parts along dimension 0
The draws below stay inside these ranges and needn't reach their ends.
There are 2 independent parts, one for each index of `groups`. The reference program is written for one: setup_inputs(seed, part) draws one part's arguments, and reference() takes and returns one part's arrays. A program takes and returns all parts, laid end to end along the dimension named above; an argument that names none is the same for every part. Nothing has to cross between parts.
All inputs are finite; a program needn't handle non-finite values.
Results may differ from the reference program's by a relative error of at most 0.0051.
Values may be sent and summed in bfloat16 or wider, within the bound.
A program may use at most 128 MiB of HBM per device.

```python
import math
import jax
import jax.numpy as jnp
from jax import lax

C = 384
H_ROWS = 4
WID = 64
CLIPS = 2
FRAMES = 8
PIXELS = 256


def with_spikes(entries, stream_key, source, target, shards_of, factor):
    def block_of(axis_at):
        return (jnp.arange(entries.shape[axis_at]) // (entries.shape[axis_at] // shards_of)).reshape((-1,) + (1,) * (entries.ndim - 1 - axis_at))

    first = jax.random.permutation(stream_key, shards_of)[block_of(target)]
    far = (block_of(target) + shards_of // 2) % shards_of
    return jnp.where((block_of(source) == first) | (block_of(source) == far), factor * entries, entries)


def block_levels(key, extent, shards, least, high):
    gain, own = 1.0, jax.random.fold_in(key, 6)
    for position, shards_of in shards:
        draws = jnp.exp(jax.random.uniform(jax.random.fold_in(own, position), (shards_of,), jnp.float32, least / len(shards), high / len(shards)))
        gain = gain * jnp.repeat(draws, extent[position] // shards_of).reshape([-1 if axis == position else 1 for axis in range(len(extent))])
    return gain


def gaussian(stream_key, shape, scale, limit, pieces=(), kind=jnp.bfloat16):
    loudness = block_levels(stream_key, shape, pieces, -0.22, 0.18) if pieces else 1.0
    drawn = jax.random.normal(stream_key, shape, jnp.float32) * scale * loudness
    return jnp.minimum(jnp.maximum(drawn, -limit), limit).astype(kind)


def gaussian_with(rng, extent, scale, reach, shards, heavy, kind=jnp.bfloat16):
    array = scale * jax.random.normal(rng, extent, jnp.float32)
    if shards:
        array = array * block_levels(rng, extent, shards, -0.22, 0.18)
    return jnp.clip(with_spikes(array, jax.random.fold_in(rng, 3), *heavy), -reach, reach).astype(kind)


def setup_inputs(seed: int = 0, part: int = 0) -> dict:
    streams_of = jax.random.split(jax.random.key(seed), 4)
    part_keys = jax.random.split(jax.random.fold_in(streams_of[3], part), 4)
    features = gaussian(part_keys[0], (C, CLIPS, FRAMES, PIXELS), 1.0, 6.0, ((0, 4), (1, 2), (2, 2)))
    kernel = gaussian_with(streams_of[1], (C, 27, C), (27 * C) ** -0.5, 0.078125, ((0, 4),), (0, 2, 4, 2.0))
    cotangent = gaussian(part_keys[2], (C, CLIPS, FRAMES, PIXELS), 1.0, 6.0, ((0, 4), (1, 2), (2, 2)))
    return {"features": features, "kernel": kernel, "cotangent": cotangent}


def reference(features, kernel, cotangent):
    widened = features.astype(jnp.float32)
    logistic = jax.nn.sigmoid(widened)
    activation = lax.optimization_barrier((widened * logistic).astype(jnp.bfloat16)).astype(jnp.float32)
    slope_factor = logistic * (1.0 + widened * (1.0 - logistic))
    grid_shape = (C, CLIPS, FRAMES, H_ROWS, WID)
    activation_grid = jnp.pad(activation.reshape(grid_shape), ((0, 0), (0, 0), (2, 0), (1, 1), (1, 1)))
    cotangent_wide = cotangent.astype(jnp.float32)
    cotangent_grid = jnp.pad(cotangent_wide.reshape(grid_shape), ((0, 0), (0, 0), (0, 2), (1, 1), (1, 1)))
    cotangent_rows = cotangent_wide.reshape(C, -1)
    kernel_wide = kernel.astype(jnp.float32)
    out_sum = jnp.zeros((C, CLIPS * FRAMES * PIXELS), jnp.float32)
    before_slope = jnp.zeros((C, CLIPS * FRAMES * PIXELS), jnp.float32)
    grad_parts = []
    for temporal in range(3):
        for vertical in range(3):
            for horizontal in range(3):
                tap_index = 9 * temporal + 3 * vertical + horizontal
                tap_matrix = kernel_wide[:, tap_index, :]
                shifted = activation_grid[:, :, temporal:temporal + FRAMES, vertical:vertical + H_ROWS, horizontal:horizontal + WID].reshape(C, -1)
                out_sum = out_sum + jnp.dot(tap_matrix, shifted, preferred_element_type=jnp.float32)
                grad_parts.append(jnp.dot(cotangent_rows, shifted.T, preferred_element_type=jnp.float32))
                flipped = cotangent_grid[:, :, 2 - temporal:2 - temporal + FRAMES, 2 - vertical:2 - vertical + H_ROWS, 2 - horizontal:2 - horizontal + WID].reshape(C, -1)
                before_slope = before_slope + jnp.dot(tap_matrix.T, flipped, preferred_element_type=jnp.float32)
    grad_scale = 1.0 / math.sqrt(CLIPS * FRAMES * PIXELS)
    conv_out = out_sum.reshape(features.shape).astype(jnp.bfloat16)
    feature_grad = (before_slope.reshape(features.shape) * slope_factor).astype(jnp.bfloat16)
    kernel_grad = jnp.stack(grad_parts, axis=1) * grad_scale
    return (conv_out, feature_grad, kernel_grad)
```

```python
import functools
import math

import jax
import jax.numpy as jnp
from jax import lax
from jax.experimental import pallas as pl
from jax.experimental.pallas import tpu as pltpu
from jax.sharding import PartitionSpec as P

WID = 64


def from_behind(x, axis, by):
    size = lax.axis_size(axis)
    pairs = [(i, i + by) for i in range(size) if 0 <= i + by < size]
    return lax.ppermute(x, axis, pairs)


def padded_copies(block):
    pixels = block.shape[-1]
    column = lax.broadcasted_iota(jnp.int32, (pixels,), 0) % WID
    nothing = jnp.zeros((), block.dtype)
    widths = [(0, 0), (0, 0), (0, 0), (WID + 1, WID + 1)]
    left_cut = jnp.pad(jnp.where(column == WID - 1, nothing, block), widths)
    untouched = jnp.pad(block, widths)
    right_cut = jnp.pad(jnp.where(column == 0, nothing, block), widths)
    return (left_cut, untouched, right_cut)


def tap_window(copies, first_frame, vertical, horizontal, frames, pixels):
    source = copies[horizontal]
    offset = vertical * WID + horizontal
    return source[:, :, first_frame : first_frame + frames, offset : offset + pixels]


def stacked_taps(copies, first_frame, flipped, frames, pixels):
    pieces = []
    for vertical in range(3):
        for horizontal in range(3):
            if flipped:
                pieces.append(
                    tap_window(copies, first_frame, 2 - vertical, 2 - horizontal, frames, pixels)
                )
            else:
                pieces.append(tap_window(copies, first_frame, vertical, horizontal, frames, pixels))
    concatenated = jnp.concatenate(pieces, axis=0)
    return concatenated.reshape(concatenated.shape[0], -1)


def local(features, kernel, cotangent):
    channels, clip_count, frames, pixels = features.shape
    flat_length = clip_count * frames * pixels
    widened = features.astype(jnp.float32)
    logistic = jax.nn.sigmoid(widened)
    activation = (widened * logistic).astype(jnp.bfloat16)
    slope_factor = logistic * (1.0 + widened * (1.0 - logistic))
    earlier = from_behind(activation[:, :, frames - 2 :, :], "tm", 1)
    extended = jnp.concatenate([earlier, activation], axis=2)
    upcoming = from_behind(cotangent[:, :, :2, :], "tm", -1)
    later_padded = jnp.concatenate([cotangent, upcoming], axis=2)
    cotangent_rows = cotangent.reshape(channels, -1)
    portion = lax.all_gather(extended, "chan", axis=0, tiled=True)
    out_sum = jnp.zeros((channels, flat_length), jnp.float32)
    amount = portion.shape[0]
    copies = padded_copies(portion)
    kernel_cols = kernel
    grad_parts = []
    for forward_temporal in range(3):
        stacked = stacked_taps(copies, forward_temporal, False, frames, pixels)
        weights = kernel_cols[:, 9 * forward_temporal : 9 * forward_temporal + 9, :].reshape(
            channels, 9 * amount
        )
        out_sum = out_sum + jnp.dot(weights, stacked, preferred_element_type=jnp.float32)
        grad_parts.append(
            lax.dot_general(
                cotangent_rows,
                stacked,
                (((1,), (1,)), ((), ())),
                preferred_element_type=jnp.float32,
            ).reshape(channels, 9, amount)
        )
    grad_sum = jnp.concatenate(grad_parts, axis=1)
    out_sum, grad_sum = (out_sum, grad_sum)
    conv_out = out_sum.reshape(features.shape).astype(jnp.bfloat16)
    position_count = lax.axis_size("dp") * lax.axis_size("tm") * flat_length
    kernel_grad = lax.psum(grad_sum, ("tm", "dp")) * (1.0 / math.sqrt(position_count))
    padded_later = padded_copies(later_padded)
    later_stacks = [
        stacked_taps(padded_later, 2 - temporal, True, frames, pixels) for temporal in range(3)
    ]
    amount = channels * lax.axis_size("chan")
    kernel_cols = kernel
    summed = jnp.zeros((amount, flat_length), jnp.float32)
    for temporal in range(3):
        weights = jnp.transpose(
            kernel_cols[:, 9 * temporal : 9 * temporal + 9, :], (2, 1, 0)
        ).reshape(amount, 9 * channels)
        summed = summed + jnp.dot(
            weights, later_stacks[temporal], preferred_element_type=jnp.float32
        )
    before_slope = lax.psum_scatter(
        summed.reshape(amount, clip_count, frames, pixels), "chan", scatter_dimension=0, tiled=True
    )
    feature_grad = (before_slope * slope_factor).astype(jnp.bfloat16)
    return (conv_out, feature_grad, kernel_grad)


def moved(x, rows, columns, pixels):
    step = rows * WID + columns
    place = lax.broadcasted_iota(jnp.int32, x.shape, len(x.shape) - 1)
    row, column = place // WID + rows, place % WID + columns
    out = x if step == 0 else pltpu.roll(x, (-step) % pixels, len(x.shape) - 1)
    inside = None
    if rows:
        inside = (row >= 0) & (row < pixels // WID)
    if columns:
        within = (column >= 0) & (column < WID)
        inside = within if inside is None else inside & within
    return out if inside is None else jnp.where(inside, out, 0.0)


def silu(x):
    wide = x.astype(jnp.float32)
    return wide * jax.nn.sigmoid(wide)


def body(
    sizes,
    f_ref, w_ref, g_ref,
    out_ref, fg_ref, kg_ref,
    halo, stack, turned, gathered, act, part, share, half_out, half_in, sum_out, sum_in, taps, edge_out, edge_in,
    gather_send, gather_recv, halo_send, halo_recv, share_send, share_recv,
    half_send, half_recv, sum_send, sum_recv, done_send, done_recv, edge_send, edge_recv,
):
    n, tm, scale = sizes
    frames, c, pixels = f_ref.shape
    full = c * n
    half = c // 2
    long = frames * pixels
    z, t, d = lax.axis_index("chan"), lax.axis_index("tm"), lax.axis_index("dp")

    def remote(src, dst, send, recv, **where):
        return pltpu.make_async_remote_copy(
            src_ref=src, dst_ref=dst, send_sem=send, recv_sem=recv,
            device_id=where, device_id_type=pl.DeviceIdType.MESH,
        )

    barrier = pltpu.get_barrier_semaphore()
    for k in range(1, n):
        pl.semaphore_signal(barrier, inc=1, device_id={"chan": lax.rem(z + k, n)}, device_id_type=pl.DeviceIdType.MESH)
    pl.semaphore_signal(barrier, inc=1, device_id={"tm": 1 - t}, device_id_type=pl.DeviceIdType.MESH)
    pl.semaphore_signal(barrier, inc=1, device_id={"dp": 1 - d}, device_id_type=pl.DeviceIdType.MESH)
    pl.semaphore_wait(barrier, n + 1)

    def gather_to(k):
        return remote(
            f_ref, gathered.at[k - 1], gather_send.at[k - 1], gather_recv.at[k - 1], chan=lax.rem(z + k, n)
        )

    def halo_copy():
        return remote(g_ref.at[pl.ds(0, 2)], halo, halo_send, halo_recv, tm=1 - t)

    @pl.when(t == 1)
    def _():
        halo_copy().start()

    for k in range(1, n):
        gather_to(k).start()

    def stack_frame(x, s):
        wide = x.astype(jnp.float32)
        for i in range(3):
            for j in range(3):
                stack[3 * i + j, :, pl.ds(pl.multiple_of(s * pixels, pixels), pixels)] = moved(
                    wide, 1 - i, 1 - j, pixels
                ).astype(jnp.bfloat16)

    def own_frame(s, _):
        stack_frame(g_ref[s], s)
        return 0

    lax.fori_loop(0, frames, own_frame, 0)

    @pl.when(t == 0)
    def _():
        halo_copy().wait_recv()

        def next_frame(s, _):
            stack_frame(halo[s], frames + s)
            return 0

        lax.fori_loop(0, 2, next_frame, 0)

    @pl.when(t == 1)
    def _():
        stack[:, :, long : long + 2 * pixels] = jnp.zeros((9, c, 2 * pixels), jnp.bfloat16)
        halo_copy().wait_send()

    def turn(a, _):
        turned[a] = jnp.transpose(w_ref[pl.ds(9 * a, 9)].reshape(9 * c, full))
        return 0

    lax.fori_loop(0, 3, turn, 0)

    def share_to(k, s):
        peer = lax.rem(z + k, n)
        return remote(
            part.at[s, pl.ds(pl.multiple_of(peer * c, c), c)], share.at[k - 1, s],
            share_send.at[k - 1, s], share_recv.at[k - 1, s], chan=peer,
        )

    def before(s, _):
        total = jnp.zeros((full, pixels), jnp.float32)
        for a in range(3):
            lanes = pl.ds(pl.multiple_of((s + 2 - a) * pixels, pixels), pixels)
            total = total + jnp.dot(
                turned[a], stack[:, :, lanes].reshape(9 * c, pixels), preferred_element_type=jnp.float32
            )
        part[s] = total.astype(jnp.bfloat16)
        for k in range(1, n):
            share_to(k, s).start()
        return 0

    lax.fori_loop(0, frames, before, 0)

    for k in range(n):
        origin = pl.ds(pl.multiple_of(lax.rem(z + n - k, n) * c, c), c)
        if k:
            gather_to(k).wait_recv()
        for s in range(frames):
            block = gathered[k - 1, s] if k else f_ref[s]
            act[origin, s * pixels : (s + 1) * pixels] = silu(block).astype(jnp.bfloat16)

    def half_rows(which):
        return pl.ds(pl.multiple_of(which * half, half), half)

    def half_copy(a):
        return remote(half_out.at[a], half_in.at[a], half_send.at[a], half_recv.at[a], tm=1 - t)

    def sum_copy(a):
        return remote(sum_out.at[a], sum_in.at[a], sum_send.at[a], sum_recv.at[a], dp=1 - d)

    def kernel_terms(a, which):
        lanes = pl.ds(pl.multiple_of((2 - a) * pixels, pixels), long)
        rows = stack[:, half_rows(which), lanes].reshape(9 * half, long)
        return lax.dot_general(
            rows, act[...], (((1,), (1,)), ((), ())), preferred_element_type=jnp.float32
        ).reshape(9, half, full)

    def terms(a, _):
        half_out[a] = kernel_terms(a, 1 - t).astype(jnp.bfloat16)
        half_copy(a).start()
        mine = kernel_terms(a, t)
        half_copy(a).wait_recv()
        sum_out[a] = (mine + half_in[a].astype(jnp.float32)).astype(jnp.bfloat16)
        sum_copy(a).start()
        return 0

    lax.fori_loop(0, 3, terms, 0)

    def edge_copy():
        return remote(edge_out, edge_in, edge_send, edge_recv, tm=1 - t)

    def convolved(u):
        total = None
        for a in range(3):
            s = u + a - 2
            if 0 <= s < frames:
                term = jnp.dot(
                    w_ref[9 * a : 9 * a + 9].reshape(9 * c, full),
                    act[:, s * pixels : (s + 1) * pixels],
                    preferred_element_type=jnp.float32,
                )
                total = term if total is None else total + term
        taps[...] = total.reshape(9, c, pixels)
        result = jnp.zeros((c, pixels), jnp.float32)
        for i in range(3):
            for j in range(3):
                result = result + moved(taps[3 * i + j], i - 1, j - 1, pixels)
        return result

    @pl.when(t == 0)
    def _():
        for u in range(2):
            edge_out[u] = convolved(frames + u)
        edge_copy().start()

    for u in list(range(2, frames)):
        out_ref[u] = convolved(u).astype(jnp.bfloat16)
    for u in range(2):
        taps_sum = convolved(u)

        @pl.when(t == 0)
        def _():
            out_ref[u] = taps_sum.astype(jnp.bfloat16)

        @pl.when(t == 1)
        def _():
            if u == 0:
                edge_copy().wait_recv()
            out_ref[u] = (taps_sum + edge_in[u]).astype(jnp.bfloat16)

    def done_copy(a):
        place = kg_ref.at[pl.ds(9 * a, 9), half_rows(t)]
        return remote(place, place, done_send.at[a], done_recv.at[a], tm=1 - t)

    def finish(a, _):
        sum_copy(a).wait_recv()
        kg_ref[pl.ds(9 * a, 9), half_rows(t)] = (
            sum_out[a].astype(jnp.float32) + sum_in[a].astype(jnp.float32)
        ) * scale
        done_copy(a).start()
        return 0

    lax.fori_loop(0, 3, finish, 0)

    def slope_frame(s, _):
        total = part[s, pl.ds(pl.multiple_of(z * c, c), c)].astype(jnp.float32)
        for k in range(1, n):
            share_to(k, s).wait_recv()
            total = total + share[k - 1, s].astype(jnp.float32)
        wide = f_ref[s].astype(jnp.float32)
        logistic = jax.nn.sigmoid(wide)
        fg_ref[s] = (total * (logistic * (1.0 + wide * (1.0 - logistic)))).astype(jnp.bfloat16)
        return 0

    lax.fori_loop(0, frames, slope_frame, 0)

    def drain_shares(s, _):
        for k in range(1, n):
            share_to(k, s).wait_send()
        return 0

    lax.fori_loop(0, frames, drain_shares, 0)
    for k in range(1, n):
        gather_to(k).wait_send()

    @pl.when(t == 0)
    def _():
        edge_copy().wait_send()

    def drain_terms(a, _):
        half_copy(a).wait_send()
        sum_copy(a).wait_send()
        done_copy(a).wait()
        return 0

    lax.fori_loop(0, 3, drain_terms, 0)


def fits(mesh, features, kernel):
    c, clips, frames, pixels = features.shape
    return (
        mesh.shape["tm"] == 2
        and mesh.shape["dp"] == 2
        and clips == 1
        and frames >= 2
        and c % 32 == 0
        and kernel.shape[2] % 128 == 0
        and pixels % 128 == 0
        and pixels % WID == 0
        and c * mesh.shape["chan"] == kernel.shape[2]
        and kernel.size * 14 + features.size * 64 < 48 * 2**20
    )


def fused(mesh, features, kernel, cotangent):
    c, clips, frames, pixels = features.shape
    n = mesh.shape["chan"]
    full = c * n
    scale = 1.0 / math.sqrt(mesh.shape["dp"] * mesh.shape["tm"] * clips * frames * pixels)
    by_frame = lambda x: jnp.transpose(x.reshape(c, frames, pixels), (1, 0, 2))
    back = lambda x: jnp.transpose(x, (1, 0, 2)).reshape(c, clips, frames, pixels)
    vmem = pl.BlockSpec(memory_space=pltpu.VMEM)
    b16, f32 = jnp.bfloat16, jnp.float32
    dma = pltpu.SemaphoreType.DMA
    half = c // 2
    halves = pltpu.VMEM((3, 9, half, full), b16)
    conv_out, feature_grad, kernel_grad = pl.pallas_call(
        functools.partial(body, (n, mesh.shape["tm"], scale)),
        out_shape=(
            jax.ShapeDtypeStruct((frames, c, pixels), b16),
            jax.ShapeDtypeStruct((frames, c, pixels), b16),
            jax.ShapeDtypeStruct((27, c, full), f32),
        ),
        in_specs=[vmem] * 3,
        out_specs=(vmem,) * 3,
        scratch_shapes=[
            pltpu.VMEM((2, c, pixels), b16),
            pltpu.VMEM((9, c, (frames + 2) * pixels), b16),
            pltpu.VMEM((3, full, 9 * c), b16),
            pltpu.VMEM((n - 1, frames, c, pixels), b16),
            pltpu.VMEM((full, frames * pixels), b16),
            pltpu.VMEM((frames, full, pixels), b16),
            pltpu.VMEM((n - 1, frames, c, pixels), b16),
            halves, halves, halves, halves,
            pltpu.VMEM((9, c, pixels), f32),
            pltpu.VMEM((2, c, pixels), f32),
            pltpu.VMEM((2, c, pixels), f32),
            dma((n - 1,)), dma((n - 1,)), dma, dma,
            dma((n - 1, frames)), dma((n - 1, frames)),
            dma((3,)), dma((3,)), dma((3,)), dma((3,)), dma((3,)), dma((3,)), dma, dma,
        ],
        compiler_params=pltpu.CompilerParams(
            collective_id=0, has_side_effects=True, vmem_limit_bytes=56 * 2**20
        ),
        name="video_conv",
    )(by_frame(features), jnp.transpose(kernel, (1, 0, 2)), by_frame(cotangent))
    return back(conv_out), back(feature_grad), jnp.transpose(kernel_grad, (1, 0, 2))


def solution(mesh):
    def chosen(features, kernel, cotangent):
        if fits(mesh, features, kernel):
            return fused(mesh, features, kernel, cotangent)
        return local(features, kernel, cotangent)

    return jax.shard_map(
        chosen,
        mesh=mesh,
        in_specs=(
            P("chan", ("groups", "dp"), "tm", None),
            P("chan", None, None),
            P("chan", ("groups", "dp"), "tm", None),
        ),
        out_specs=(
            P("chan", ("groups", "dp"), "tm", None),
            P("chan", ("groups", "dp"), "tm", None),
            P(("groups", "chan"), None, None),
        ),
        check_vma=False,
    )
```

```python
import functools
import math

import jax
import jax.numpy as jnp
from jax import lax
from jax.experimental import pallas as pl
from jax.experimental.pallas import tpu as pltpu
from jax.sharding import PartitionSpec as P

WID = 64


def from_behind(x, axis, by):
    size = lax.axis_size(axis)
    pairs = [(i, i + by) for i in range(size) if 0 <= i + by < size]
    return lax.ppermute(x, axis, pairs)


def padded_copies(block):
    pixels = block.shape[-1]
    column = lax.broadcasted_iota(jnp.int32, (pixels,), 0) % WID
    nothing = jnp.zeros((), block.dtype)
    widths = [(0, 0), (0, 0), (0, 0), (WID + 1, WID + 1)]
    left_cut = jnp.pad(jnp.where(column == WID - 1, nothing, block), widths)
    untouched = jnp.pad(block, widths)
    right_cut = jnp.pad(jnp.where(column == 0, nothing, block), widths)
    return (left_cut, untouched, right_cut)


def tap_window(copies, first_frame, vertical, horizontal, frames, pixels):
    source = copies[horizontal]
    offset = vertical * WID + horizontal
    return source[:, :, first_frame : first_frame + frames, offset : offset + pixels]


def stacked_taps(copies, first_frame, flipped, frames, pixels):
    pieces = []
    for vertical in range(3):
        for horizontal in range(3):
            if flipped:
                pieces.append(
                    tap_window(copies, first_frame, 2 - vertical, 2 - horizontal, frames, pixels)
                )
            else:
                pieces.append(tap_window(copies, first_frame, vertical, horizontal, frames, pixels))
    concatenated = jnp.concatenate(pieces, axis=0)
    return concatenated.reshape(concatenated.shape[0], -1)


def local(features, kernel, cotangent):
    channels, clip_count, frames, pixels = features.shape
    flat_length = clip_count * frames * pixels
    widened = features.astype(jnp.float32)
    logistic = jax.nn.sigmoid(widened)
    activation = (widened * logistic).astype(jnp.bfloat16)
    slope_factor = logistic * (1.0 + widened * (1.0 - logistic))
    earlier = from_behind(activation[:, :, frames - 2 :, :], "tm", 1)
    extended = jnp.concatenate([earlier, activation], axis=2)
    upcoming = from_behind(cotangent[:, :, :2, :], "tm", -1)
    later_padded = jnp.concatenate([cotangent, upcoming], axis=2)
    cotangent_rows = cotangent.reshape(channels, -1)
    portion = lax.all_gather(extended, "chan", axis=0, tiled=True)
    out_sum = jnp.zeros((channels, flat_length), jnp.float32)
    amount = portion.shape[0]
    copies = padded_copies(portion)
    kernel_cols = kernel
    grad_parts = []
    for forward_temporal in range(3):
        stacked = stacked_taps(copies, forward_temporal, False, frames, pixels)
        weights = kernel_cols[:, 9 * forward_temporal : 9 * forward_temporal + 9, :].reshape(
            channels, 9 * amount
        )
        out_sum = out_sum + jnp.dot(weights, stacked, preferred_element_type=jnp.float32)
        grad_parts.append(
            lax.dot_general(
                cotangent_rows,
                stacked,
                (((1,), (1,)), ((), ())),
                preferred_element_type=jnp.float32,
            ).reshape(channels, 9, amount)
        )
    grad_sum = jnp.concatenate(grad_parts, axis=1)
    out_sum, grad_sum = (out_sum, grad_sum)
    conv_out = out_sum.reshape(features.shape).astype(jnp.bfloat16)
    position_count = lax.axis_size("dp") * lax.axis_size("tm") * flat_length
    kernel_grad = lax.psum(grad_sum, ("tm", "dp")) * (1.0 / math.sqrt(position_count))
    padded_later = padded_copies(later_padded)
    later_stacks = [
        stacked_taps(padded_later, 2 - temporal, True, frames, pixels) for temporal in range(3)
    ]
    amount = channels * lax.axis_size("chan")
    kernel_cols = kernel
    summed = jnp.zeros((amount, flat_length), jnp.float32)
    for temporal in range(3):
        weights = jnp.transpose(
            kernel_cols[:, 9 * temporal : 9 * temporal + 9, :], (2, 1, 0)
        ).reshape(amount, 9 * channels)
        summed = summed + jnp.dot(
            weights, later_stacks[temporal], preferred_element_type=jnp.float32
        )
    before_slope = lax.psum_scatter(
        summed.reshape(amount, clip_count, frames, pixels), "chan", scatter_dimension=0, tiled=True
    )
    feature_grad = (before_slope * slope_factor).astype(jnp.bfloat16)
    return (conv_out, feature_grad, kernel_grad)


def moved(x, rows, columns, pixels):
    step = rows * WID + columns
    place = lax.broadcasted_iota(jnp.int32, x.shape, len(x.shape) - 1)
    row, column = place // WID + rows, place % WID + columns
    out = x if step == 0 else pltpu.roll(x, (-step) % pixels, len(x.shape) - 1)
    inside = None
    if rows:
        inside = (row >= 0) & (row < pixels // WID)
    if columns:
        within = (column >= 0) & (column < WID)
        inside = within if inside is None else inside & within
    return out if inside is None else jnp.where(inside, out, 0.0)


def silu(x):
    wide = x.astype(jnp.float32)
    return wide * jax.nn.sigmoid(wide)


def body(
    sizes,
    f_ref, w_ref, g_ref,
    out_ref, fg_ref, kg_ref,
    halo, stack, turned, gathered, act, part, right_in, left_in, half_out, half_in, sum_out, sum_in, taps, edge_out, edge_in,
    gather_right, gather_left, gather_recv, halo_send, halo_recv, right_send, right_recv, left_send, left_recv,
    half_send, half_recv, sum_send, sum_recv, done_send, done_recv, edge_send, edge_recv,
):
    n, lanes = sizes
    frames, c, pixels = f_ref.shape
    full = c * n
    half = c // 2
    long = frames * pixels
    groups = full // lanes
    z, t, d = lax.axis_index("chan"), lax.axis_index("tm"), lax.axis_index("dp")

    def remote(src, dst, send, recv, **where):
        return pltpu.make_async_remote_copy(
            src_ref=src, dst_ref=dst, send_sem=send, recv_sem=recv,
            device_id=where, device_id_type=pl.DeviceIdType.MESH,
        )

    barrier = pltpu.get_barrier_semaphore()

    def greet(**where):
        pl.semaphore_signal(barrier, inc=1, device_id=where, device_id_type=pl.DeviceIdType.MESH)

    greet(tm=1 - t)
    greet(dp=1 - d)

    for k in range(1, n):
        greet(chan=lax.rem(z + k, n))
    pl.semaphore_wait(barrier, n + 1)

    def shard(q):
        return gathered.at[q]

    def pass_right(k):
        q = z - k
        return remote(f_ref if k == 0 else shard(q), shard(q), gather_right.at[k], gather_recv.at[q], chan=z + 1)

    def pass_left(k):
        q = z + k
        return remote(f_ref if k == 0 else shard(q), shard(q), gather_left.at[k], gather_recv.at[q], chan=z - 1)

    def arrival(q):
        return remote(shard(q), shard(q), gather_right.at[0], gather_recv.at[q], chan=lax.rem(z + 1, n))

    def halo_copy():
        return remote(g_ref.at[pl.ds(0, 2)], halo, halo_send, halo_recv, tm=1 - t)

    @pl.when(z < n - 1)
    def _():
        pass_right(0).start()

    @pl.when(z > 0)
    def _():
        pass_left(0).start()

    @pl.when(t == 1)
    def _():
        halo_copy().start()

    def activate(block, q):
        for s in range(frames):
            act[pl.ds(pl.multiple_of(q * c, c), c), s * pixels : (s + 1) * pixels] = silu(block[s]).astype(jnp.bfloat16)

    def stack_frame(x, s):
        wide = x.astype(jnp.float32)
        for i in range(3):
            for j in range(3):
                stack[3 * i + j, :, pl.ds(pl.multiple_of(s * pixels, pixels), pixels)] = moved(
                    wide, 1 - i, 1 - j, pixels
                ).astype(jnp.bfloat16)

    def own_frame(s, _):
        stack_frame(g_ref[s], s)
        return 0

    lax.fori_loop(0, frames, own_frame, 0)

    @pl.when(t == 0)
    def _():
        halo_copy().wait_recv()

        def next_frame(s, _):
            stack_frame(halo[s], frames + s)
            return 0

        lax.fori_loop(0, 2, next_frame, 0)

    @pl.when(t == 1)
    def _():
        stack[:, :, long : long + 2 * pixels] = jnp.zeros((9, c, 2 * pixels), jnp.bfloat16)
        halo_copy().wait_send()

    activate(f_ref, z)

    def turn(a, _):
        turned[a] = jnp.transpose(w_ref[pl.ds(9 * a, 9)].reshape(9 * c, full))
        return 0

    lax.fori_loop(0, 3, turn, 0)

    def arrive(k):
        @pl.when(z >= k)
        def _():
            arrival(z - k).wait_recv()

            @pl.when(z < n - 1)
            def _():
                pass_right(k).start()

        @pl.when(z + k < n)
        def _():
            arrival(z + k).wait_recv()

            @pl.when(z > 0)
            def _():
                pass_left(k).start()

        @pl.when(z >= k)
        def _():
            activate(shard(z - k), z - k)

        @pl.when(z + k < n)
        def _():
            activate(shard(z + k), z + k)

    def half_rows(which):
        return pl.ds(pl.multiple_of(which * half, half), half)

    def group_at(i):
        return pl.ds(pl.multiple_of((i + (2 * z // n) * (groups - 1 - 2 * i)) * lanes, lanes), lanes)

    def half_copy(m):
        return remote(half_out.at[m], half_in.at[m], half_send.at[m], half_recv.at[m], tm=1 - t)

    def sum_copy(m):
        return remote(sum_out.at[m], sum_in.at[m], sum_send.at[m], sum_recv.at[m], dp=1 - d)

    def kernel_terms(i, a, which):
        span = pl.ds(pl.multiple_of((2 - a) * pixels, pixels), long)
        rows = stack[:, half_rows(which), span].reshape(9 * half, long)
        return lax.dot_general(
            rows, act[group_at(i), :], (((1,), (1,)), ((), ())), preferred_element_type=jnp.float32
        ).reshape(9, half, lanes)

    def group_terms(i):
        def theirs(a, _):
            half_out[3 * i + a] = kernel_terms(i, a, 1 - t).astype(jnp.bfloat16)
            half_copy(3 * i + a).start()
            return 0

        lax.fori_loop(0, 3, theirs, 0)

        def ours(a, _):
            m = 3 * i + a
            mine = kernel_terms(i, a, t)
            half_copy(m).wait_recv()
            sum_out[m] = (mine + half_in[m].astype(jnp.float32)).astype(jnp.bfloat16)
            sum_copy(m).start()
            return 0

        lax.fori_loop(0, 3, ours, 0)

    def share_right(q, src):
        return remote(src.at[q], right_in.at[q], right_send.at[q], right_recv.at[q], chan=z + 1)

    def share_left(q, src):
        return remote(src.at[q], left_in.at[q], left_send.at[q], left_recv.at[q], chan=z - 1)

    def before(s, _):
        total = jnp.zeros((full, pixels), jnp.float32)
        for a in range(3):
            span = pl.ds(pl.multiple_of((s + 2 - a) * pixels, pixels), pixels)
            total = total + jnp.dot(
                turned[a], stack[:, :, span].reshape(9 * c, pixels), preferred_element_type=jnp.float32
            )
        for q in range(n):
            part[q, s] = total[q * c : (q + 1) * c].astype(jnp.bfloat16)
        return 0

    def add_part(held, q):
        for s in range(frames):
            held[q, s] = (held[q, s].astype(jnp.float32) + part[q, s].astype(jnp.float32)).astype(jnp.bfloat16)

    def first_shares():
        for j in range(n - 1):
            @pl.when(z == 0)
            def _():
                share_right(n - 1 - j, part).start()

            @pl.when(z == n - 1)
            def _():
                share_left(j, part).start()

    def wait_share(held, q, sem):
        remote(held.at[q], held.at[q], right_send.at[q], sem.at[q], chan=lax.rem(z + 1, n)).wait_recv()

    def relay(j):
        @pl.when((z > 0) & (z < n - 1 - j))
        def _():
            wait_share(right_in, n - 1 - j, right_recv)
            add_part(right_in, n - 1 - j)
            share_right(n - 1 - j, right_in).start()

        @pl.when((z < n - 1) & (z > j))
        def _():
            wait_share(left_in, j, left_recv)
            add_part(left_in, j)
            share_left(j, left_in).start()

    def ready_after(i):
        first, last = i * lanes // c, ((i + 1) * lanes - 1) // c
        return max(max(abs(at - first), abs(at - last)) for at in range((n + 1) // 2))

    arrived = 0
    for i in range(groups):
        while arrived < ready_after(i):
            arrived += 1
            arrive(arrived)
        group_terms(i)
        if i == 0:
            lax.fori_loop(0, frames, before, 0)
            first_shares()
    while arrived < n - 1:
        arrived += 1
        arrive(arrived)

    def edge_copy():
        return remote(edge_out, edge_in, edge_send, edge_recv, tm=1 - t)

    def convolved(u):
        total = None
        for a in range(3):
            s = u + a - 2
            if 0 <= s < frames:
                term = jnp.dot(
                    w_ref[9 * a : 9 * a + 9].reshape(9 * c, full),
                    act[:, s * pixels : (s + 1) * pixels],
                    preferred_element_type=jnp.float32,
                )
                total = term if total is None else total + term
        taps[...] = total.reshape(9, c, pixels)
        result = jnp.zeros((c, pixels), jnp.float32)
        for i in range(3):
            for j in range(3):
                result = result + moved(taps[3 * i + j], i - 1, j - 1, pixels)
        return result

    relay(0)

    @pl.when(t == 0)
    def _():
        for u in range(2):
            edge_out[u] = convolved(frames + u)
        edge_copy().start()

    later = list(range(2, frames)) + [0, 1]
    for step, u in enumerate(later):
        value = convolved(u)
        if u >= 2:
            out_ref[u] = value.astype(jnp.bfloat16)
        else:
            @pl.when(t == 0)
            def _():
                out_ref[u] = value.astype(jnp.bfloat16)

            @pl.when(t == 1)
            def _():
                if u == 0:
                    edge_copy().wait_recv()
                out_ref[u] = (value + edge_in[u]).astype(jnp.bfloat16)
        if step + 1 < n - 1:
            relay(step + 1)
    for j in range(len(later) + 1, n - 1):
        relay(j)

    def done_copy(i, a):
        place = kg_ref.at[pl.ds(9 * a, 9), half_rows(t), group_at(i)]
        return remote(place, place, done_send.at[3 * i + a], done_recv.at[3 * i + a], tm=1 - t)

    def finish(i):
        def one(a, _):
            m = 3 * i + a
            sum_copy(m).wait_recv()
            kg_ref[pl.ds(9 * a, 9), half_rows(t), group_at(i)] = (
                sum_out[m].astype(jnp.float32) + sum_in[m].astype(jnp.float32)
            ).astype(jnp.bfloat16)
            done_copy(i, a).start()
            return 0

        lax.fori_loop(0, 3, one, 0)

    for i in range(groups - 1):
        finish(i)

    @pl.when(z > 0)
    def _():
        wait_share(right_in, z, right_recv)

    @pl.when(z < n - 1)
    def _():
        wait_share(left_in, z, left_recv)

    def slope_frame(s, _):
        wide = f_ref[s].astype(jnp.float32)
        logistic = jax.nn.sigmoid(wide)
        slope = logistic * (1.0 + wide * (1.0 - logistic))

        def keep(total):
            fg_ref[s] = (total * slope).astype(jnp.bfloat16)

        own = part[z, s].astype(jnp.float32)

        @pl.when(z == 0)
        def _():
            keep(own + left_in[z, s].astype(jnp.float32))

        @pl.when(z == n - 1)
        def _():
            keep(own + right_in[z, s].astype(jnp.float32))

        @pl.when((z > 0) & (z < n - 1))
        def _():
            keep(own + (left_in[z, s].astype(jnp.float32) + right_in[z, s].astype(jnp.float32)))

        return 0

    lax.fori_loop(0, frames, slope_frame, 0)
    finish(groups - 1)

    for k in range(n - 1):
        @pl.when((z < n - 1) & (z >= k))
        def _():
            pass_right(k).wait_send()

        @pl.when((z > 0) & (z + k < n))
        def _():
            pass_left(k).wait_send()

    for j in range(n - 1):
        @pl.when(z < n - 1 - j)
        def _():
            share_right(n - 1 - j, right_in).wait_send()

        @pl.when(z > j)
        def _():
            share_left(j, left_in).wait_send()

    @pl.when(t == 0)
    def _():
        edge_copy().wait_send()

    for i in range(groups):
        def drain(a, _):
            half_copy(3 * i + a).wait_send()
            sum_copy(3 * i + a).wait_send()
            done_copy(i, a).wait()
            return 0

        lax.fori_loop(0, 3, drain, 0)


def fits(mesh, features, kernel):
    c, clips, frames, pixels = features.shape
    return (
        mesh.shape["tm"] == 2
        and mesh.shape["chan"] >= 2
        and mesh.shape["dp"] == 2
        and clips == 1
        and frames >= 2
        and c % 32 == 0
        and kernel.shape[2] % 128 == 0
        and pixels % 128 == 0
        and pixels % WID == 0
        and c * mesh.shape["chan"] == kernel.shape[2]
        and kernel.size * 14 + features.size * 64 < 48 * 2**20
    )


def fused(mesh, features, kernel, cotangent):
    c, clips, frames, pixels = features.shape
    n = mesh.shape["chan"]
    full = c * n
    scale = 1.0 / math.sqrt(mesh.shape["dp"] * mesh.shape["tm"] * clips * frames * pixels)
    by_frame = lambda x: jnp.transpose(x.reshape(c, frames, pixels), (1, 0, 2))
    back = lambda x: jnp.transpose(x, (1, 0, 2)).reshape(c, clips, frames, pixels)
    vmem = pl.BlockSpec(memory_space=pltpu.VMEM)
    b16, f32 = jnp.bfloat16, jnp.float32
    dma = pltpu.SemaphoreType.DMA
    half = c // 2
    lanes = 128
    pieces = 3 * (full // lanes)
    halves = pltpu.VMEM((pieces, 9, half, lanes), b16)
    shards = pltpu.VMEM((n, frames, c, pixels), b16)
    conv_out, feature_grad, kernel_grad = pl.pallas_call(
        functools.partial(body, (n, lanes)),
        out_shape=(
            jax.ShapeDtypeStruct((frames, c, pixels), b16),
            jax.ShapeDtypeStruct((frames, c, pixels), b16),
            jax.ShapeDtypeStruct((27, c, full), b16),
        ),
        in_specs=[vmem] * 3,
        out_specs=(vmem,) * 3,
        scratch_shapes=[
            pltpu.VMEM((2, c, pixels), b16),
            pltpu.VMEM((9, c, (frames + 2) * pixels), b16),
            pltpu.VMEM((3, full, 9 * c), b16),
            shards,
            pltpu.VMEM((full, frames * pixels), b16),
            shards, shards, shards,
            halves, halves, halves, halves,
            pltpu.VMEM((9, c, pixels), f32),
            pltpu.VMEM((2, c, pixels), f32),
            pltpu.VMEM((2, c, pixels), f32),
            dma((n,)), dma((n,)), dma((n,)), dma, dma,
            dma((n,)), dma((n,)), dma((n,)), dma((n,)),
            dma((pieces,)), dma((pieces,)), dma((pieces,)), dma((pieces,)), dma((pieces,)), dma((pieces,)), dma, dma,
        ],
        compiler_params=pltpu.CompilerParams(
            collective_id=0, has_side_effects=True, vmem_limit_bytes=56 * 2**20
        ),
        name="video_conv",
    )(by_frame(features), jnp.transpose(kernel, (1, 0, 2)), by_frame(cotangent))
    kernel_grad = jnp.transpose(kernel_grad, (1, 0, 2)).astype(f32) * scale
    return back(conv_out), back(feature_grad), kernel_grad


def solution(mesh):
    def chosen(features, kernel, cotangent):
        if fits(mesh, features, kernel):
            return fused(mesh, features, kernel, cotangent)
        return local(features, kernel, cotangent)

    return jax.shard_map(
        chosen,
        mesh=mesh,
        in_specs=(
            P("chan", ("groups", "dp"), "tm", None),
            P("chan", None, None),
            P("chan", ("groups", "dp"), "tm", None),
        ),
        out_specs=(
            P("chan", ("groups", "dp"), "tm", None),
            P("chan", ("groups", "dp"), "tm", None),
            P(("groups", "chan"), None, None),
        ),
        check_vma=False,
    )
```

```python
import functools
import math

import jax
import jax.numpy as jnp
from jax import lax
from jax.experimental import pallas as pl
from jax.experimental.pallas import tpu as pltpu
from jax.sharding import PartitionSpec as P

WID = 64


def from_behind(x, axis, by):
    size = lax.axis_size(axis)
    pairs = [(i, i + by) for i in range(size) if 0 <= i + by < size]
    return lax.ppermute(x, axis, pairs)


def padded_copies(block):
    pixels = block.shape[-1]
    column = lax.broadcasted_iota(jnp.int32, (pixels,), 0) % WID
    nothing = jnp.zeros((), block.dtype)
    widths = [(0, 0), (0, 0), (0, 0), (WID + 1, WID + 1)]
    left_cut = jnp.pad(jnp.where(column == WID - 1, nothing, block), widths)
    untouched = jnp.pad(block, widths)
    right_cut = jnp.pad(jnp.where(column == 0, nothing, block), widths)
    return (left_cut, untouched, right_cut)


def tap_window(copies, first_frame, vertical, horizontal, frames, pixels):
    source = copies[horizontal]
    offset = vertical * WID + horizontal
    return source[:, :, first_frame : first_frame + frames, offset : offset + pixels]


def stacked_taps(copies, first_frame, flipped, frames, pixels):
    pieces = []
    for vertical in range(3):
        for horizontal in range(3):
            if flipped:
                pieces.append(
                    tap_window(copies, first_frame, 2 - vertical, 2 - horizontal, frames, pixels)
                )
            else:
                pieces.append(tap_window(copies, first_frame, vertical, horizontal, frames, pixels))
    concatenated = jnp.concatenate(pieces, axis=0)
    return concatenated.reshape(concatenated.shape[0], -1)


def local(features, kernel, cotangent):
    channels, clip_count, frames, pixels = features.shape
    flat_length = clip_count * frames * pixels
    widened = features.astype(jnp.float32)
    logistic = jax.nn.sigmoid(widened)
    activation = (widened * logistic).astype(jnp.bfloat16)
    slope_factor = logistic * (1.0 + widened * (1.0 - logistic))
    earlier = from_behind(activation[:, :, frames - 2 :, :], "tm", 1)
    extended = jnp.concatenate([earlier, activation], axis=2)
    upcoming = from_behind(cotangent[:, :, :2, :], "tm", -1)
    later_padded = jnp.concatenate([cotangent, upcoming], axis=2)
    cotangent_rows = cotangent.reshape(channels, -1)
    portion = lax.all_gather(extended, "chan", axis=0, tiled=True)
    out_sum = jnp.zeros((channels, flat_length), jnp.float32)
    amount = portion.shape[0]
    copies = padded_copies(portion)
    kernel_cols = kernel
    grad_parts = []
    for forward_temporal in range(3):
        stacked = stacked_taps(copies, forward_temporal, False, frames, pixels)
        weights = kernel_cols[:, 9 * forward_temporal : 9 * forward_temporal + 9, :].reshape(
            channels, 9 * amount
        )
        out_sum = out_sum + jnp.dot(weights, stacked, preferred_element_type=jnp.float32)
        grad_parts.append(
            lax.dot_general(
                cotangent_rows,
                stacked,
                (((1,), (1,)), ((), ())),
                preferred_element_type=jnp.float32,
            ).reshape(channels, 9, amount)
        )
    grad_sum = jnp.concatenate(grad_parts, axis=1)
    out_sum, grad_sum = (out_sum, grad_sum)
    conv_out = out_sum.reshape(features.shape).astype(jnp.bfloat16)
    position_count = lax.axis_size("dp") * lax.axis_size("tm") * flat_length
    kernel_grad = lax.psum(grad_sum, ("tm", "dp")) * (1.0 / math.sqrt(position_count))
    padded_later = padded_copies(later_padded)
    later_stacks = [
        stacked_taps(padded_later, 2 - temporal, True, frames, pixels) for temporal in range(3)
    ]
    amount = channels * lax.axis_size("chan")
    kernel_cols = kernel
    summed = jnp.zeros((amount, flat_length), jnp.float32)
    for temporal in range(3):
        weights = jnp.transpose(
            kernel_cols[:, 9 * temporal : 9 * temporal + 9, :], (2, 1, 0)
        ).reshape(amount, 9 * channels)
        summed = summed + jnp.dot(
            weights, later_stacks[temporal], preferred_element_type=jnp.float32
        )
    before_slope = lax.psum_scatter(
        summed.reshape(amount, clip_count, frames, pixels), "chan", scatter_dimension=0, tiled=True
    )
    feature_grad = (before_slope * slope_factor).astype(jnp.bfloat16)
    return (conv_out, feature_grad, kernel_grad)


def moved(x, rows, columns, pixels):
    step = rows * WID + columns
    place = lax.broadcasted_iota(jnp.int32, x.shape, len(x.shape) - 1)
    row, column = place // WID + rows, place % WID + columns
    out = x if step == 0 else pltpu.roll(x, (-step) % pixels, len(x.shape) - 1)
    inside = None
    if rows:
        inside = (row >= 0) & (row < pixels // WID)
    if columns:
        within = (column >= 0) & (column < WID)
        inside = within if inside is None else inside & within
    return out if inside is None else jnp.where(inside, out, 0.0)


def silu(x):
    wide = x.astype(jnp.float32)
    return wide * jax.nn.sigmoid(wide)


def body(
    sizes,
    f_ref, w_ref, g_ref,
    out_ref, fg_ref, kg_ref,
    halo, stack, turned, gathered, act, part, right_in, left_in, half_out, half_in, sum_out, sum_in, taps, edge_out, edge_in,
    gather_right, gather_left, gather_recv, halo_send, halo_recv, right_send, right_recv, left_send, left_recv,
    half_send, half_recv, sum_send, sum_recv, done_send, done_recv, edge_send, edge_recv,
):
    n, lanes = sizes
    frames, c, pixels = f_ref.shape
    full = c * n
    half = c // 2
    long = frames * pixels
    groups = full // lanes
    z, t, d = lax.axis_index("chan"), lax.axis_index("tm"), lax.axis_index("dp")

    def remote(src, dst, send, recv, **where):
        return pltpu.make_async_remote_copy(
            src_ref=src, dst_ref=dst, send_sem=send, recv_sem=recv,
            device_id=where, device_id_type=pl.DeviceIdType.MESH,
        )

    barrier = pltpu.get_barrier_semaphore()

    def greet(**where):
        pl.semaphore_signal(barrier, inc=1, device_id=where, device_id_type=pl.DeviceIdType.MESH)

    greet(tm=1 - t)
    greet(dp=1 - d)

    for k in range(1, n):
        greet(chan=lax.rem(z + k, n))
    pl.semaphore_wait(barrier, n + 1)

    def shard(q):
        return gathered.at[q]

    def pass_right(k):
        q = z - k
        return remote(f_ref if k == 0 else shard(q), shard(q), gather_right.at[k], gather_recv.at[q], chan=z + 1)

    def pass_left(k):
        q = z + k
        return remote(f_ref if k == 0 else shard(q), shard(q), gather_left.at[k], gather_recv.at[q], chan=z - 1)

    def arrival(q):
        return remote(shard(q), shard(q), gather_right.at[0], gather_recv.at[q], chan=lax.rem(z + 1, n))

    def halo_copy():
        return remote(g_ref.at[pl.ds(0, 2)], halo, halo_send, halo_recv, tm=1 - t)

    @pl.when(z < n - 1)
    def _():
        pass_right(0).start()

    @pl.when(z > 0)
    def _():
        pass_left(0).start()

    @pl.when(t == 1)
    def _():
        halo_copy().start()

    def activate(block, q):
        for s in range(frames):
            act[pl.ds(pl.multiple_of(q * c, c), c), s * pixels : (s + 1) * pixels] = silu(block[s]).astype(jnp.bfloat16)

    def stack_frame(x, s):
        wide = x.astype(jnp.float32)
        for i in range(3):
            for j in range(3):
                stack[3 * i + j, :, pl.ds(pl.multiple_of(s * pixels, pixels), pixels)] = moved(
                    wide, 1 - i, 1 - j, pixels
                ).astype(jnp.bfloat16)

    def own_frame(s, _):
        stack_frame(g_ref[s], s)
        return 0

    lax.fori_loop(0, frames, own_frame, 0)

    @pl.when(t == 0)
    def _():
        halo_copy().wait_recv()

        def next_frame(s, _):
            stack_frame(halo[s], frames + s)
            return 0

        lax.fori_loop(0, 2, next_frame, 0)

    @pl.when(t == 1)
    def _():
        stack[:, :, long : long + 2 * pixels] = jnp.zeros((9, c, 2 * pixels), jnp.bfloat16)
        halo_copy().wait_send()

    activate(f_ref, z)

    def turn(a, _):
        turned[a] = jnp.transpose(w_ref[pl.ds(9 * a, 9)].reshape(9 * c, full))
        return 0

    lax.fori_loop(0, 3, turn, 0)

    def arrive(k):
        @pl.when(z >= k)
        def _():
            arrival(z - k).wait_recv()

            @pl.when(z < n - 1)
            def _():
                pass_right(k).start()

        @pl.when(z + k < n)
        def _():
            arrival(z + k).wait_recv()

            @pl.when(z > 0)
            def _():
                pass_left(k).start()

        @pl.when(z >= k)
        def _():
            activate(shard(z - k), z - k)

        @pl.when(z + k < n)
        def _():
            activate(shard(z + k), z + k)

    def half_rows(which):
        return pl.ds(pl.multiple_of(which * half, half), half)

    def group_at(i):
        return pl.ds(pl.multiple_of((i + (2 * z // n) * (groups - 1 - 2 * i)) * lanes, lanes), lanes)

    def half_copy(m):
        return remote(half_out.at[m], half_in.at[m], half_send.at[m], half_recv.at[m], tm=1 - t)

    def sum_copy(m):
        return remote(sum_out.at[m], sum_in.at[m], sum_send.at[m], sum_recv.at[m], dp=1 - d)

    def kernel_terms(i, a, which):
        span = pl.ds(pl.multiple_of((2 - a) * pixels, pixels), long)
        rows = stack[:, half_rows(which), span].reshape(9 * half, long)
        return lax.dot_general(
            rows, act[group_at(i), :], (((1,), (1,)), ((), ())), preferred_element_type=jnp.float32
        ).reshape(9, half, lanes)

    def group_terms(i):
        def theirs(a, _):
            half_out[3 * i + a] = kernel_terms(i, a, 1 - t).astype(jnp.bfloat16)
            half_copy(3 * i + a).start()
            return 0

        lax.fori_loop(0, 3, theirs, 0)

        def ours(a, _):
            m = 3 * i + a
            mine = kernel_terms(i, a, t)
            half_copy(m).wait_recv()
            sum_out[m] = (mine + half_in[m].astype(jnp.float32)).astype(jnp.bfloat16)
            sum_copy(m).start()
            return 0

        lax.fori_loop(0, 3, ours, 0)

    def share_right(q, src):
        return remote(src.at[q], right_in.at[q], right_send.at[q], right_recv.at[q], chan=z + 1)

    def share_left(q, src):
        return remote(src.at[q], left_in.at[q], left_send.at[q], left_recv.at[q], chan=z - 1)

    def before(s, _):
        total = jnp.zeros((full, pixels), jnp.float32)
        for a in range(3):
            span = pl.ds(pl.multiple_of((s + 2 - a) * pixels, pixels), pixels)
            total = total + jnp.dot(
                turned[a], stack[:, :, span].reshape(9 * c, pixels), preferred_element_type=jnp.float32
            )
        for q in range(n):
            part[q, s] = total[q * c : (q + 1) * c].astype(jnp.bfloat16)
        return 0

    def add_part(held, q):
        for s in range(frames):
            held[q, s] = (held[q, s].astype(jnp.float32) + part[q, s].astype(jnp.float32)).astype(jnp.bfloat16)

    def first_shares():
        for j in range(n - 1):
            @pl.when(z == 0)
            def _():
                share_right(n - 1 - j, part).start()

            @pl.when(z == n - 1)
            def _():
                share_left(j, part).start()

    def wait_share(held, q, sem):
        remote(held.at[q], held.at[q], right_send.at[q], sem.at[q], chan=lax.rem(z + 1, n)).wait_recv()

    def relay_right(j, ahead):
        @pl.when((z > 0) & (z < n - 1 - j) & ahead)
        def _():
            wait_share(right_in, n - 1 - j, right_recv)
            add_part(right_in, n - 1 - j)
            share_right(n - 1 - j, right_in).start()

    def relay_left(j, ahead):
        @pl.when((z < n - 1) & (z > j) & ahead)
        def _():
            wait_share(left_in, j, left_recv)
            add_part(left_in, j)
            share_left(j, left_in).start()

    def relay(j):
        lower = 2 * z < n
        if j < n - 1:
            relay_right(j, lower)
            relay_left(j, jnp.logical_not(lower))
        if j > 0:
            relay_right(j - 1, jnp.logical_not(lower))
            relay_left(j - 1, lower)

    def ready_after(i):
        first, last = i * lanes // c, ((i + 1) * lanes - 1) // c
        return max(max(abs(at - first), abs(at - last)) for at in range((n + 1) // 2))

    arrived = 0
    for i in range(groups):
        while arrived < ready_after(i):
            arrived += 1
            arrive(arrived)
        group_terms(i)
        if i == 0:
            lax.fori_loop(0, frames, before, 0)
            first_shares()
    while arrived < n - 1:
        arrived += 1
        arrive(arrived)

    def edge_copy():
        return remote(edge_out, edge_in, edge_send, edge_recv, tm=1 - t)

    def convolved(u):
        total = None
        for a in range(3):
            s = u + a - 2
            if 0 <= s < frames:
                term = jnp.dot(
                    w_ref[9 * a : 9 * a + 9].reshape(9 * c, full),
                    act[:, s * pixels : (s + 1) * pixels],
                    preferred_element_type=jnp.float32,
                )
                total = term if total is None else total + term
        taps[...] = total.reshape(9, c, pixels)
        result = jnp.zeros((c, pixels), jnp.float32)
        for i in range(3):
            for j in range(3):
                result = result + moved(taps[3 * i + j], i - 1, j - 1, pixels)
        return result

    relay(0)

    @pl.when(t == 0)
    def _():
        for u in range(2):
            edge_out[u] = convolved(frames + u)
        edge_copy().start()

    later = list(range(2, frames)) + [0, 1]
    for step, u in enumerate(later):
        value = convolved(u)
        if u >= 2:
            out_ref[u] = value.astype(jnp.bfloat16)
        else:
            @pl.when(t == 0)
            def _():
                out_ref[u] = value.astype(jnp.bfloat16)

            @pl.when(t == 1)
            def _():
                if u == 0:
                    edge_copy().wait_recv()
                out_ref[u] = (value + edge_in[u]).astype(jnp.bfloat16)
        if step + 1 < n:
            relay(step + 1)
    for j in range(len(later) + 1, n):
        relay(j)

    def done_copy(i, a):
        place = kg_ref.at[pl.ds(9 * a, 9), half_rows(t), group_at(i)]
        return remote(place, place, done_send.at[3 * i + a], done_recv.at[3 * i + a], tm=1 - t)

    def finish(i):
        def one(a, _):
            m = 3 * i + a
            sum_copy(m).wait_recv()
            kg_ref[pl.ds(9 * a, 9), half_rows(t), group_at(i)] = (
                sum_out[m].astype(jnp.float32) + sum_in[m].astype(jnp.float32)
            ).astype(jnp.bfloat16)
            done_copy(i, a).start()
            return 0

        lax.fori_loop(0, 3, one, 0)

    for i in range(groups - 1):
        finish(i)

    @pl.when(z > 0)
    def _():
        wait_share(right_in, z, right_recv)

    @pl.when(z < n - 1)
    def _():
        wait_share(left_in, z, left_recv)

    def slope_frame(s, _):
        wide = f_ref[s].astype(jnp.float32)
        logistic = jax.nn.sigmoid(wide)
        slope = logistic * (1.0 + wide * (1.0 - logistic))

        def keep(total):
            fg_ref[s] = (total * slope).astype(jnp.bfloat16)

        own = part[z, s].astype(jnp.float32)

        @pl.when(z == 0)
        def _():
            keep(own + left_in[z, s].astype(jnp.float32))

        @pl.when(z == n - 1)
        def _():
            keep(own + right_in[z, s].astype(jnp.float32))

        @pl.when((z > 0) & (z < n - 1))
        def _():
            keep(own + (left_in[z, s].astype(jnp.float32) + right_in[z, s].astype(jnp.float32)))

        return 0

    lax.fori_loop(0, frames, slope_frame, 0)
    finish(groups - 1)

    for k in range(n - 1):
        @pl.when((z < n - 1) & (z >= k))
        def _():
            pass_right(k).wait_send()

        @pl.when((z > 0) & (z + k < n))
        def _():
            pass_left(k).wait_send()

    for j in range(n - 1):
        @pl.when(z < n - 1 - j)
        def _():
            share_right(n - 1 - j, right_in).wait_send()

        @pl.when(z > j)
        def _():
            share_left(j, left_in).wait_send()

    @pl.when(t == 0)
    def _():
        edge_copy().wait_send()

    for i in range(groups):
        def drain(a, _):
            half_copy(3 * i + a).wait_send()
            sum_copy(3 * i + a).wait_send()
            done_copy(i, a).wait()
            return 0

        lax.fori_loop(0, 3, drain, 0)


def fits(mesh, features, kernel):
    c, clips, frames, pixels = features.shape
    return (
        mesh.shape["tm"] == 2
        and mesh.shape["chan"] >= 2
        and mesh.shape["dp"] == 2
        and clips == 1
        and frames >= 2
        and c % 32 == 0
        and kernel.shape[2] % 128 == 0
        and pixels % 128 == 0
        and pixels % WID == 0
        and c * mesh.shape["chan"] == kernel.shape[2]
        and kernel.size * 14 + features.size * 64 < 48 * 2**20
    )


def fused(mesh, features, kernel, cotangent):
    c, clips, frames, pixels = features.shape
    n = mesh.shape["chan"]
    full = c * n
    scale = 1.0 / math.sqrt(mesh.shape["dp"] * mesh.shape["tm"] * clips * frames * pixels)
    by_frame = lambda x: jnp.transpose(x.reshape(c, frames, pixels), (1, 0, 2))
    back = lambda x: jnp.transpose(x, (1, 0, 2)).reshape(c, clips, frames, pixels)
    vmem = pl.BlockSpec(memory_space=pltpu.VMEM)
    b16, f32 = jnp.bfloat16, jnp.float32
    dma = pltpu.SemaphoreType.DMA
    half = c // 2
    lanes = 128
    pieces = 3 * (full // lanes)
    limit = 8 * 2**20 + kernel.size * 14 + features.size * 64
    halves = pltpu.VMEM((pieces, 9, half, lanes), b16)
    shards = pltpu.VMEM((n, frames, c, pixels), b16)
    conv_out, feature_grad, kernel_grad = pl.pallas_call(
        functools.partial(body, (n, lanes)),
        out_shape=(
            jax.ShapeDtypeStruct((frames, c, pixels), b16),
            jax.ShapeDtypeStruct((frames, c, pixels), b16),
            jax.ShapeDtypeStruct((27, c, full), b16),
        ),
        in_specs=[vmem] * 3,
        out_specs=(vmem,) * 3,
        scratch_shapes=[
            pltpu.VMEM((2, c, pixels), b16),
            pltpu.VMEM((9, c, (frames + 2) * pixels), b16),
            pltpu.VMEM((3, full, 9 * c), b16),
            shards,
            pltpu.VMEM((full, frames * pixels), b16),
            shards, shards, shards,
            halves, halves, halves, halves,
            pltpu.VMEM((9, c, pixels), f32),
            pltpu.VMEM((2, c, pixels), f32),
            pltpu.VMEM((2, c, pixels), f32),
            dma((n,)), dma((n,)), dma((n,)), dma, dma,
            dma((n,)), dma((n,)), dma((n,)), dma((n,)),
            dma((pieces,)), dma((pieces,)), dma((pieces,)), dma((pieces,)), dma((pieces,)), dma((pieces,)), dma, dma,
        ],
        compiler_params=pltpu.CompilerParams(
            collective_id=0, has_side_effects=True, vmem_limit_bytes=limit
        ),
        name="video_conv",
    )(by_frame(features), jnp.transpose(kernel, (1, 0, 2)), by_frame(cotangent))
    kernel_grad = jnp.transpose(kernel_grad, (1, 0, 2)).astype(f32) * scale
    return back(conv_out), back(feature_grad), kernel_grad


def solution(mesh):
    def chosen(features, kernel, cotangent):
        if fits(mesh, features, kernel):
            return fused(mesh, features, kernel, cotangent)
        return local(features, kernel, cotangent)

    return jax.shard_map(
        chosen,
        mesh=mesh,
        in_specs=(
            P("chan", ("groups", "dp"), "tm", None),
            P("chan", None, None),
            P("chan", ("groups", "dp"), "tm", None),
        ),
        out_specs=(
            P("chan", ("groups", "dp"), "tm", None),
            P("chan", ("groups", "dp"), "tm", None),
            P(("groups", "chan"), None, None),
        ),
        check_vma=False,
    )
```
